32 devices in a mesh: fsdp: 2 (over y), context: 4 (over x, core), tensor: 4 (over z).
Axes of the slice: x: 2, y: 2, z: 4, core: 2. Of those that a mesh axis runs over, the one named last changes fastest.
Arguments:
- layer_input: float32 [2048, 2048], P(('fsdp', 'context')), may hold values from -6 to 6
- doc_lengths: int32 [2, 3], P('fsdp'), may hold values from 1 to 512, 1024 in all within a row
- ln_gain: float32 [2, 2048], replicated, may hold values from 0.5 to 1.5
- ln_shift: float32 [2, 2048], replicated, may hold values from -3 to 3
- qkv_weight: bfloat16 [2, 2048, 3, 2048], P(None, ('fsdp', 'context'), None, 'tensor'), as said below
- qkv_bias: float32 [2, 3, 2048], P(None, None, 'tensor'), may hold values from -3 to 3
- out_weight: bfloat16 [2, 2048, 2048], P(None, 'tensor', ('fsdp', 'context')), may hold values from -0.5 to 0.5
- out_bias: float32 [2, 2048], replicated, may hold values from -3 to 3
- fc1_weight: bfloat16 [2, 2048, 8192], P(None, ('fsdp', 'context'), 'tensor'), may hold values from -0.125 to 0.125
- fc1_bias: float32 [2, 8192], P(None, 'tensor'), may hold values from -3 to 3
- fc2_weight: bfloat16 [2, 8192, 2048], P(None, 'tensor', ('fsdp', 'context')), may hold values from -0.0625 to 0.0625
- fc2_bias: float32 [2, 2048], replicated, may hold values from -3 to 3
- cotangent: float32 [2048, 2048], P(('fsdp', 'context')), may hold values from -6 to 6
Outputs:
- layer_output: float32 [2048, 2048], P(('fsdp', 'context'))
- input_grad: float32 [2048, 2048], P(('fsdp', 'context'))
- ln_gain_grad: float32 [2, 2048], replicated
- ln_shift_grad: float32 [2, 2048], replicated
- qkv_weight_grad: float32 [2, 2048, 3, 2048], P(None, ('fsdp', 'context'), None, 'tensor')
- qkv_bias_grad: float32 [2, 3, 2048], P(None, None, 'tensor')
- out_weight_grad: float32 [2, 2048, 2048], P(None, 'tensor', ('fsdp', 'context'))
- out_bias_grad: float32 [2, 2048], replicated
- fc1_weight_grad: float32 [2, 2048, 8192], P(None, ('fsdp', 'context'), 'tensor')
- fc1_bias_grad: float32 [2, 8192], P(None, 'tensor')
- fc2_weight_grad: float32 [2, 8192, 2048], P(None, 'tensor', ('fsdp', 'context'))
- fc2_bias_grad: float32 [2, 2048], replicated
The draws below stay inside these ranges and needn't reach their ends.
Inputs may be any that keep to these rules, and one draw needn't show every extreme that they name: `doc_lengths`: each row holds the lengths of its pack's documents in order; they sum to 1024 and the largest is exactly 512. `qkv_weight`: key and value entries have mean 0 and a spread of about 2048 ** -0.5. The query weights of a head are either alike, or a multiple (up to about 40) of that head's key weights plus independent entries of 0.3 times that spread, so that scores can reach several hundred.
All inputs are finite; a program needn't handle non-finite values.
Results may differ from the reference program's by a relative error of at most 0.015.
The reference program's roundings to bfloat16 on the way count: a program that leaves them out, or rounds other values in their place, can miss the bound.
Values may be sent and summed in bfloat16 or wider, within the bound.
No kernel may reach another device: no remote copies, remote signals or barrier semaphores. Data moves between devices by JAX's collectives and lax.ppermute only.
A program may use at most 320 MiB of HBM per device.

```python
import math
import jax
import jax.numpy as jnp
import numpy as np
from jax import lax

D = 2048
HEADS = 32
HEAD = 64
ROT = 32
FF = 8192
LAYERS = 2
DOCS = 3
GROUP_TOK = 1024
DOC_MOST = 512
GROUPS = 2
TOKENS = 2048


def draw_qkv_weight(key, part):
    base_draw = jax.random.normal(jax.random.fold_in(key, 11), (LAYERS, D, 3, D), jnp.float32) * D ** (-0.5)
    return base_draw.astype(jnp.bfloat16)


def levels(rng, shape, pieces, least, top_value):
    def one(axis_at, shards_of):
        draws = jax.random.uniform(jax.random.fold_in(jax.random.fold_in(rng, 6), axis_at), (shards_of,), jnp.float32, least / len(pieces), top_value / len(pieces))
        return jnp.repeat(jnp.exp(draws), shape[axis_at] // shards_of).reshape((-1,) + (1,) * (len(shape) - axis_at - 1))

    factor_of = one(*pieces[0])
    for cut in pieces[1:]:
        factor_of = factor_of * one(*cut)
    return factor_of


def profile(amount, total, limit, slope):
    loads = [(1 << 20) // math.isqrt(grade ** slope) + 1 for grade in range(2, amount + 1)]
    rest, counts = total - limit - (amount - 1), [1] * (amount - 1)
    while rest > 0:
        free = [i for i in range(amount - 1) if counts[i] < limit]
        pool, budget = sum([loads[i] for i in free]), rest
        for i in free:
            extra = min(limit - counts[i], max(1, budget * loads[i] // pool), rest)
            counts[i] = counts[i] + extra
            rest = rest - extra
    return np.array([limit] + counts)


def ragged(rng, count, total, bound, lean):
    if count == 2:
        one = jax.random.randint(rng, (), max(1, total - bound), min(bound, total - 1) + 1)
        return jnp.stack([one, total - one])
    sizes = jnp.asarray(profile(count, total, bound, lean), jnp.int32)
    pairs = (count - 1) // 2
    source_of, taker = sizes[1:1 + 2 * pairs:2], sizes[2:2 + 2 * pairs:2]
    room = jnp.minimum(source_of - 1, bound - taker)
    shifted = jax.random.randint(jax.random.fold_in(rng, 1), (pairs,), 0, 1 << 20) % (room + 1)
    sizes = sizes.at[1:1 + 2 * pairs:2].set(source_of - shifted).at[2:2 + 2 * pairs:2].set(taker + shifted)
    return sizes[jax.random.permutation(jax.random.fold_in(rng, 2), count)]


def scatter_about(key, shape, width, most, split=(), kind=jnp.bfloat16):
    array = width * jax.random.normal(key, shape, jnp.float32)
    if split:
        array = array * levels(key, shape, split, -0.22, 0.18)
    return jnp.clip(array, -most, most).astype(kind)


def setup_inputs(seed: int = 0) -> dict:
    splits = jax.random.split(jax.random.key(seed), 14)
    layer_input = scatter_about(splits[0], (TOKENS, D), 1.0, 6.0, ((0, 8),), jnp.float32)
    doc_lengths = jax.vmap(lambda own: ragged(own, DOCS, GROUP_TOK, DOC_MOST, 2))(jax.random.split(splits[1], GROUPS)).reshape((GROUPS, DOCS)).astype(jnp.int32)
    ln_gain = jnp.clip(1.0 + 0.1 * jax.random.normal(splits[2], (LAYERS, D), jnp.float32), 0.5, 1.5)
    ln_shift = scatter_about(splits[3], (LAYERS, D), 0.5, 3.0, (), jnp.float32)
    qkv_weight = draw_qkv_weight(jax.random.fold_in(splits[13], 71), 0)
    qkv_bias = scatter_about(splits[5], (LAYERS, 3, D), 0.5, 3.0, ((2, 4),), jnp.float32)
    out_weight = scatter_about(splits[6], (LAYERS, D, D), (D // 16) ** -0.5, 0.5, ((1, 4), (2, 8)))
    out_bias = scatter_about(splits[7], (LAYERS, D), 0.5, 3.0, (), jnp.float32)
    fc1_weight = scatter_about(splits[8], (LAYERS, D, FF), D ** -0.5, 0.125, ((1, 8), (2, 4)))
    fc1_bias = scatter_about(splits[9], (LAYERS, FF), 0.5, 3.0, ((1, 4),), jnp.float32)
    fc2_weight = scatter_about(splits[10], (LAYERS, FF, D), FF ** -0.5, 0.0625, ((1, 4), (2, 8)))
    fc2_bias = scatter_about(splits[11], (LAYERS, D), 0.5, 3.0, (), jnp.float32)
    cotangent = scatter_about(splits[12], (TOKENS, D), 1.0, 6.0, ((0, 8),), jnp.float32)
    return dict(layer_input=layer_input, doc_lengths=doc_lengths, ln_gain=ln_gain, ln_shift=ln_shift, qkv_weight=qkv_weight, qkv_bias=qkv_bias, out_weight=out_weight, out_bias=out_bias, fc1_weight=fc1_weight, fc1_bias=fc1_bias, fc2_weight=fc2_weight, fc2_bias=fc2_bias, cotangent=cotangent)


LN_EPS = 1e-05
ROPE_BASE = 10000.0
GELU_SCALE = 0.7978845608028654
GELU_CUBIC = 0.044715

def gelu_value(preact):
    return 0.5 * preact * (1.0 + jnp.tanh(GELU_SCALE * (preact + GELU_CUBIC * preact * preact * preact)))

def gelu_slope(preact):
    tanh_val = jnp.tanh(GELU_SCALE * (preact + GELU_CUBIC * preact * preact * preact))
    inner_slope = GELU_SCALE * (1.0 + 3.0 * GELU_CUBIC * preact * preact)
    return 0.5 * (1.0 + tanh_val) + 0.5 * preact * (1.0 - tanh_val * tanh_val) * inner_slope

def doc_layout(lengths, row_count):
    doc_ends = jnp.cumsum(lengths).astype(jnp.int32)
    place_ids = jnp.arange(row_count, dtype=jnp.int32)
    passed = (place_ids[:, None] >= doc_ends[None, :]).astype(jnp.int32)
    doc_id = lax.optimization_barrier(jnp.sum(passed, axis=1)).astype(jnp.int32)
    doc_start = lax.optimization_barrier(jnp.sum(passed * lengths[None, :], axis=1)).astype(jnp.int32)
    return (doc_id, place_ids - doc_start)

def rope_tables(position):
    half_rot = ROT // 2
    frequency = jnp.exp(jnp.arange(half_rot, dtype=jnp.float32) * (-2.0 * math.log(ROPE_BASE) / ROT))
    angles = position.astype(jnp.float32)[:, None] * frequency[None, :]
    return (jnp.cos(angles), jnp.sin(angles))

def rotate(values_in, cosine_tab, sine_tab, direction):
    half_rot = ROT // 2
    first_half = values_in[..., :half_rot]
    second = values_in[..., half_rot:ROT]
    cos_rows = cosine_tab[:, None, :]
    sin_rows = sine_tab[:, None, :] * direction
    return jnp.concatenate([first_half * cos_rows - second * sin_rows, second * cos_rows + first_half * sin_rows, values_in[..., ROT:]], axis=-1)

def block_mask(block_start, block_rows, doc_id, key_pos):
    query_pos = block_start + jnp.arange(block_rows, dtype=jnp.int32)
    query_doc = lax.dynamic_slice_in_dim(doc_id, block_start, block_rows, 0)
    return (key_pos[None, :] <= query_pos[:, None]) & (doc_id[None, :] == query_doc[:, None])

def attend(query_rows, key_rows, value_rows, doc_id):
    row_count = query_rows.shape[0]
    block_rows = min(512, row_count)
    key_pos = jnp.arange(row_count, dtype=jnp.int32)
    score_scale = query_rows.shape[2] ** (-0.5)
    key_wide = key_rows.astype(jnp.float32)
    value_wide = value_rows.astype(jnp.float32)

    def one_block(block_num):
        block_start = block_num * block_rows
        query_blk = lax.dynamic_slice_in_dim(query_rows, block_start, block_rows, 0).astype(jnp.float32)
        allowed = block_mask(block_start, block_rows, doc_id, key_pos)
        scores = jnp.einsum('qhd,khd->hqk', query_blk, key_wide) * score_scale
        scores = jnp.where(allowed[None], scores, -jnp.inf)
        row_max = lax.optimization_barrier(jnp.max(scores, axis=2, keepdims=True))
        log_sum = row_max + jnp.log(lax.optimization_barrier(jnp.sum(jnp.exp(scores - row_max), axis=2, keepdims=True)))
        attn_probs = jnp.exp(scores - log_sum).astype(jnp.bfloat16)
        block_out = jnp.einsum('hqk,khd->qhd', attn_probs.astype(jnp.float32), value_wide)
        return (block_out.astype(jnp.bfloat16), log_sum[:, :, 0])
    block_outs, log_sums = lax.map(one_block, jnp.arange(row_count // block_rows, dtype=jnp.int32))
    return (block_outs.reshape(query_rows.shape), log_sums)

def attend_back(query_rows, key_rows, value_rows, out_rows, out_grad, log_sums, doc_id):
    row_count = query_rows.shape[0]
    block_rows = min(512, row_count)
    key_pos = jnp.arange(row_count, dtype=jnp.int32)
    score_scale = query_rows.shape[2] ** (-0.5)
    key_wide = key_rows.astype(jnp.float32)
    value_wide = value_rows.astype(jnp.float32)
    row_delta = lax.optimization_barrier(jnp.sum(out_grad.astype(jnp.float32) * out_rows.astype(jnp.float32), axis=2))

    def one_block(carried, scan_item):
        block_num, log_sum = scan_item
        key_grad, value_grad = carried
        block_start = block_num * block_rows
        query_blk = lax.dynamic_slice_in_dim(query_rows, block_start, block_rows, 0).astype(jnp.float32)
        grad_blk = lax.dynamic_slice_in_dim(out_grad, block_start, block_rows, 0).astype(jnp.float32)
        delta_blk = lax.dynamic_slice_in_dim(row_delta, block_start, block_rows, 0)
        allowed = block_mask(block_start, block_rows, doc_id, key_pos)
        scores = jnp.einsum('qhd,khd->hqk', query_blk, key_wide) * score_scale
        scores = jnp.where(allowed[None], scores, -jnp.inf)
        attn_probs = jnp.exp(scores - log_sum[:, :, None])
        probs_low = attn_probs.astype(jnp.bfloat16).astype(jnp.float32)
        value_grad = value_grad + jnp.einsum('hqk,qhd->khd', probs_low, grad_blk)
        prob_grad = jnp.einsum('qhd,khd->hqk', grad_blk, value_wide)
        score_grad = (attn_probs * (prob_grad - delta_blk.T[:, :, None]) * score_scale).astype(jnp.bfloat16).astype(jnp.float32)
        query_grad = jnp.einsum('hqk,khd->qhd', score_grad, key_wide)
        key_grad = key_grad + jnp.einsum('hqk,qhd->khd', score_grad, query_blk)
        return ((key_grad, value_grad), query_grad)
    zero_state = jnp.zeros(query_rows.shape, jnp.float32)
    scan_items = (jnp.arange(row_count // block_rows, dtype=jnp.int32), log_sums)
    (key_grad, value_grad), query_grad = lax.scan(one_block, (zero_state, zero_state), scan_items)
    return (query_grad.reshape(query_rows.shape), key_grad, value_grad)

def contract_rows(left, right):
    return lax.dot_general(left, right, (((0,), (0,)), ((), ())), preferred_element_type=jnp.float32)

def contract_cols(left, right):
    return lax.dot_general(left, right, (((1,), (1,)), ((), ())), preferred_element_type=jnp.float32)

def reference(layer_input, doc_lengths, ln_gain, ln_shift, qkv_weight, qkv_bias, out_weight, out_bias, fc1_weight, fc1_bias, fc2_weight, fc2_bias, cotangent):
    tok_total = layer_input.shape[0]
    doc_ids, positions = jax.vmap(lambda lengths: doc_layout(lengths, GROUP_TOK))(doc_lengths)
    cosine_tab, sine_tab = rope_tables(positions.reshape(tok_total))
    grouped_shape = (GROUPS, GROUP_TOK, HEADS, HEAD)
    hidden = layer_input
    stored = []
    for layer_num in range(LAYERS):
        w_qkv = qkv_weight[layer_num].reshape(D, 3 * D)
        row_mean = lax.optimization_barrier(jnp.mean(hidden, axis=1, keepdims=True))
        centred = hidden - row_mean
        inv_std = lax.rsqrt(lax.optimization_barrier(jnp.mean(centred * centred, axis=1, keepdims=True)) + LN_EPS)
        normed = centred * inv_std
        normal_in = (normed * ln_gain[layer_num] + ln_shift[layer_num]).astype(jnp.bfloat16)
        projected = jnp.dot(normal_in, w_qkv, preferred_element_type=jnp.float32).reshape(tok_total, 3, HEADS, HEAD)
        projected = projected + qkv_bias[layer_num].reshape(3, HEADS, HEAD)
        queries = rotate(projected[:, 0], cosine_tab, sine_tab, 1.0).astype(jnp.bfloat16).reshape(grouped_shape)
        key_rot = rotate(projected[:, 1], cosine_tab, sine_tab, 1.0).astype(jnp.bfloat16).reshape(grouped_shape)
        value_rows = projected[:, 2].astype(jnp.bfloat16).reshape(grouped_shape)
        att_heads, log_sums = lax.map(lambda item_set: attend(*item_set), (queries, key_rot, value_rows, doc_ids))
        att_tok = att_heads.reshape(tok_total, D)
        preact = jnp.dot(normal_in, fc1_weight[layer_num], preferred_element_type=jnp.float32) + fc1_bias[layer_num]
        gelu_out = gelu_value(preact).astype(jnp.bfloat16)
        branch_sum = jnp.dot(att_tok, out_weight[layer_num], preferred_element_type=jnp.float32) + jnp.dot(gelu_out, fc2_weight[layer_num], preferred_element_type=jnp.float32)
        stored.append((normed, inv_std, normal_in, queries, key_rot, value_rows, att_heads, log_sums, preact, gelu_out))
        hidden = hidden + branch_sum + out_bias[layer_num] + fc2_bias[layer_num]
    upstream = cotangent
    grad_lists = [[None] * LAYERS for column in range(10)]
    for layer_num in reversed(range(LAYERS)):
        normed, inv_std, normal_in, queries, key_rot, value_rows, att_heads, log_sums, preact, gelu_out = stored[layer_num]
        upstream_low = upstream.astype(jnp.bfloat16)
        grad_obias = lax.optimization_barrier(jnp.sum(upstream, axis=0))
        grad_w2 = contract_rows(gelu_out, upstream_low)
        grad_pre = contract_cols(upstream_low, fc2_weight[layer_num]) * gelu_slope(preact)
        grad_b1 = lax.optimization_barrier(jnp.sum(grad_pre, axis=0))
        grad_pre_low = grad_pre.astype(jnp.bfloat16)
        grad_w1 = contract_rows(normal_in, grad_pre_low)
        grad_in = contract_cols(grad_pre_low, fc1_weight[layer_num])
        att_tok = att_heads.reshape(tok_total, D)
        grad_wo = contract_rows(att_tok, upstream_low)
        grad_att = contract_cols(upstream_low, out_weight[layer_num]).astype(jnp.bfloat16).reshape(grouped_shape)
        grad_q, grad_k, grad_v = lax.map(lambda item_set: attend_back(*item_set), (queries, key_rot, value_rows, att_heads, grad_att, log_sums, doc_ids))
        flat_shape = (tok_total, HEADS, HEAD)
        grad_q = rotate(grad_q.reshape(flat_shape), cosine_tab, sine_tab, -1.0)
        grad_k = rotate(grad_k.reshape(flat_shape), cosine_tab, sine_tab, -1.0)
        grad_proj = jnp.stack([grad_q, grad_k, grad_v.reshape(flat_shape)], axis=1)
        grad_qbias = lax.optimization_barrier(jnp.sum(grad_proj, axis=0)).reshape(3, D)
        grad_proj_low = grad_proj.reshape(tok_total, 3 * D).astype(jnp.bfloat16)
        grad_wqkv = contract_rows(normal_in, grad_proj_low).reshape(D, 3, D)
        grad_in = grad_in + contract_cols(grad_proj_low, qkv_weight[layer_num].reshape(D, 3 * D))
        grad_gain = lax.optimization_barrier(jnp.sum(grad_in * normed, axis=0))
        grad_shift = lax.optimization_barrier(jnp.sum(grad_in, axis=0))
        grad_normed = grad_in * ln_gain[layer_num]
        upstream = upstream + inv_std * (grad_normed - lax.optimization_barrier(jnp.mean(grad_normed, axis=1, keepdims=True)) - normed * lax.optimization_barrier(jnp.mean(grad_normed * normed, axis=1, keepdims=True)))
        found = (grad_gain, grad_shift, grad_wqkv, grad_qbias, grad_wo, grad_obias, grad_w1, grad_b1, grad_w2, grad_obias)
        for column in range(10):
            grad_lists[column][layer_num] = found[column]
    stacked = [jnp.stack(entry_list) for entry_list in grad_lists]
    return (hidden, upstream, stacked[0], stacked[1], stacked[2], stacked[3], stacked[4], stacked[5], stacked[6], stacked[7], stacked[8], stacked[9])
```

```python
import math

import jax
import jax.numpy as jnp
from jax import lax
from jax.experimental import pallas as pl
from jax.experimental.pallas import tpu as pltpu
from jax.sharding import PartitionSpec as P


HEAD = 64
ROT = 32


LN_EPS = 1e-05
ROPE_BASE = 10000.0
GELU_SCALE = 0.7978845608028654
GELU_CUBIC = 0.044715


def gelu_value(preact):
    return (
        0.5
        * preact
        * (1.0 + jnp.tanh(GELU_SCALE * (preact + GELU_CUBIC * preact * preact * preact)))
    )


def gelu_slope(preact):
    tanh_val = jnp.tanh(GELU_SCALE * (preact + GELU_CUBIC * preact * preact * preact))
    inner_slope = GELU_SCALE * (1.0 + 3.0 * GELU_CUBIC * preact * preact)
    return 0.5 * (1.0 + tanh_val) + 0.5 * preact * (1.0 - tanh_val * tanh_val) * inner_slope


def doc_layout(lengths, row_count):
    doc_ends = jnp.cumsum(lengths)
    place_ids = jnp.arange(row_count, dtype=jnp.int32)
    passed = (place_ids[:, None] >= doc_ends[None, :]).astype(jnp.int32)
    doc_id = jnp.sum(passed, axis=1)
    doc_start = jnp.sum(passed * lengths[None, :], axis=1)
    return (doc_id, place_ids - doc_start)


def rope_tables(position):
    half_rot = ROT // 2
    frequency = jnp.exp(
        jnp.arange(half_rot, dtype=jnp.float32) * (-2.0 * math.log(ROPE_BASE) / ROT)
    )
    angles = position.astype(jnp.float32)[:, None] * frequency[None, :]
    return (jnp.cos(angles), jnp.sin(angles))


def contract_rows(left, right):
    return lax.dot_general(
        left, right, (((0,), (0,)), ((), ())), preferred_element_type=jnp.float32
    )


def contract_cols(left, right):
    return lax.dot_general(
        left, right, (((1,), (1,)), ((), ())), preferred_element_type=jnp.float32
    )


def matmul(left, right):
    return jnp.dot(left, right, preferred_element_type=jnp.float32)


class Place:
    def __init__(self):
        self.F = lax.axis_size("fsdp")
        self.C = lax.axis_size("context")
        self.T = lax.axis_size("tensor")
        self.X = self.C // 2
        self.f = lax.axis_index("fsdp")
        ctx = lax.axis_index("context")
        self.hi = ctx // 2
        self.lo = ctx % 2
        self.t = lax.axis_index("tensor")

    def to_lo(self, val):
        return lax.ppermute(val, "context", [(i, i ^ 1) for i in range(self.C)])

    def to_hi(self, val, dist):
        return lax.ppermute(val, "context", [(i, i ^ (2 * dist)) for i in range(self.C)])

    def to_f(self, val, dist):
        return lax.ppermute(val, "fsdp", [(i, i ^ dist) for i in range(self.F)])

    def to_t(self, val, dist):
        return lax.ppermute(val, "tensor", [(i, i ^ dist) for i in range(self.T)])


def xor_order(parts, index):
    count = len(parts)
    bit = 1
    while bit < count:
        on = (index & bit) != 0
        parts = [jnp.where(on, parts[i ^ bit], parts[i]) for i in range(count)]
        bit *= 2
    return parts


def split_cols(val, count):
    width = val.shape[-1] // count
    return [val[..., i * width : (i + 1) * width] for i in range(count)]


def split_rows(val, count):
    height = val.shape[0] // count
    return [val[i * height : (i + 1) * height] for i in range(count)]


def rel_cols(val, place):
    chunks = split_cols(val, place.F * place.X)
    rows = [
        xor_order(chunks[i * place.X : (i + 1) * place.X], place.hi) for i in range(place.F)
    ]
    out = []
    swapped = [xor_order([rows[i][j] for i in range(place.F)], place.f) for j in range(place.X)]
    for i in range(place.F):
        for j in range(place.X):
            out.append(swapped[j][i])
    return jnp.concatenate(out, axis=-1)


def rel_rows(val, place):
    return jnp.concatenate(xor_order(split_rows(val, place.T), place.t), axis=0)


def token_index(place, rows):
    own = jnp.arange(rows, dtype=jnp.int32)
    step = rows // place.T
    inner = (place.t ^ (own // step)) * step + own % step
    out = []
    for dx in range(place.X):
        for dlo in range(2):
            out.append(((place.hi ^ dx) * 2 + (place.lo ^ dlo)) * rows + inner)
    return jnp.concatenate(out)


def rope_wide(position, heads):
    cos_tab, sin_tab = rope_tables(position)
    rows = position.shape[0]
    rest = HEAD - ROT
    cos_head = jnp.concatenate([cos_tab, cos_tab, jnp.ones((rows, rest), jnp.float32)], axis=1)
    sin_head = jnp.concatenate([-sin_tab, sin_tab, jnp.zeros((rows, rest), jnp.float32)], axis=1)
    return (jnp.tile(cos_head, (1, heads)), jnp.tile(sin_head, (1, heads)))


BLOCK = 256


def scores_by_key(qkv_ref, start, head, width, key_idx_ref, row_idx_ref, row_first_ref):
    lane = head * HEAD
    queries = qkv_ref[pl.ds(start, BLOCK), lane : lane + HEAD]
    key_rows = qkv_ref[:, width + lane : width + lane + HEAD]
    scores = contract_cols(key_rows, queries) * (HEAD**-0.5)
    key_idx = key_idx_ref[...]
    keep = (key_idx <= row_idx_ref[...]) & (key_idx >= row_first_ref[...])
    return scores, keep, queries, key_rows


def attend_kernel(qkv_ref, key_idx_ref, row_idx_ref, row_first_ref, out_ref, lse_ref):
    width = out_ref.shape[1]
    start = pl.multiple_of(pl.program_id(0) * BLOCK, BLOCK)
    for head in range(width // HEAD):
        lane = head * HEAD
        scores, keep, _, _ = scores_by_key(
            qkv_ref, start, head, width, key_idx_ref, row_idx_ref, row_first_ref
        )
        values = qkv_ref[:, 2 * width + lane : 2 * width + lane + HEAD]
        scores = jnp.where(keep, scores, -jnp.inf)
        top = jnp.max(scores, axis=0, keepdims=True)
        weight = jnp.exp(scores - top)
        total = jnp.sum(weight, axis=0, keepdims=True)
        probs = (weight * (1.0 / total)).astype(jnp.bfloat16)
        out = contract_rows(values, probs)
        out_ref[:, lane : lane + HEAD] = out.T.astype(jnp.bfloat16)
        lse_ref[head : head + 1, :] = top + jnp.log(total)


def attend(qkv, key_idx, row_idx, row_first):
    rows, cols = qkv.shape
    width = cols // 3
    whole = pl.BlockSpec((rows, cols), lambda i: (0, 0))
    row = pl.BlockSpec((1, BLOCK), lambda i: (0, i))
    return pl.pallas_call(
        attend_kernel,
        grid=(rows // BLOCK,),
        in_specs=[whole, pl.BlockSpec((rows, BLOCK), lambda i: (0, 0)), row, row],
        out_specs=[
            pl.BlockSpec((BLOCK, width), lambda i: (i, 0)),
            pl.BlockSpec((width // HEAD, BLOCK), lambda i: (0, i)),
        ],
        out_shape=[
            jax.ShapeDtypeStruct((rows, width), jnp.bfloat16),
            jax.ShapeDtypeStruct((width // HEAD, rows), jnp.float32),
        ],
        name="attend",
    )(qkv, key_idx, row_idx, row_first)


def turn(val, cos_ref, sin_ref, direction):
    half_rot = ROT // 2
    lane = lax.broadcasted_iota(jnp.int32, val.shape, 1) % HEAD
    cols = val.shape[1]
    partner = jnp.where(
        lane < half_rot, pltpu.roll(val, cols - half_rot, 1), pltpu.roll(val, half_rot, 1)
    )
    return val * cos_ref[...] + partner * (sin_ref[...] * direction)


def attend_back_kernel(
    qkv_ref, att_ref, grad_ref, lse_ref, key_idx_ref, row_idx_ref, row_first_ref, cos_ref, sin_ref,
    out_ref, bias_ref, acc_ref,
):
    width = att_ref.shape[1]
    step = pl.program_id(0)
    start = pl.multiple_of(step * BLOCK, BLOCK)
    scale = HEAD**-0.5

    @pl.when(step == 0)
    def _():
        acc_ref[...] = jnp.zeros_like(acc_ref)

    both = grad_ref[pl.ds(start, BLOCK), :].astype(jnp.float32) * att_ref[
        pl.ds(start, BLOCK), :
    ].astype(jnp.float32)
    both = both.T
    for head in range(width // HEAD):
        lane = head * HEAD
        scores, keep, queries, key_rows = scores_by_key(
            qkv_ref, start, head, width, key_idx_ref, row_idx_ref, row_first_ref
        )
        values = qkv_ref[:, 2 * width + lane : 2 * width + lane + HEAD]
        grads = grad_ref[pl.ds(start, BLOCK), lane : lane + HEAD]
        delta = jnp.sum(both[lane : lane + HEAD, :], axis=0, keepdims=True)
        probs = jnp.where(keep, jnp.exp(scores - lse_ref[head : head + 1, :]), 0.0)
        acc_ref[:, 2 * width + lane : 2 * width + lane + HEAD] += matmul(
            probs.astype(jnp.bfloat16), grads
        )
        prob_grad = contract_cols(values, grads)
        score_grad = (probs * (prob_grad - delta) * scale).astype(jnp.bfloat16)
        acc_ref[:, width + lane : width + lane + HEAD] += matmul(score_grad, queries)
        acc_ref[pl.ds(start, BLOCK), lane : lane + HEAD] = contract_rows(key_rows, score_grad).T

    @pl.when(step == pl.num_programs(0) - 1)
    def _():
        for part in range(3):
            val = acc_ref[:, part * width : (part + 1) * width]
            if part < 2:
                val = turn(val, cos_ref, sin_ref, -1.0)
            bias_ref[:, part * width : (part + 1) * width] = jnp.sum(val, axis=0, keepdims=True)
            out_ref[:, part * width : (part + 1) * width] = val.astype(jnp.bfloat16)


def attend_back(qkv, att, grads, lse, key_idx, row_idx, row_first, cos_wide, sin_wide):
    rows, cols = qkv.shape
    width = cols // 3
    whole = pl.BlockSpec((rows, cols), lambda i: (0, 0))
    part = pl.BlockSpec((rows, width), lambda i: (0, 0))
    row = pl.BlockSpec((1, BLOCK), lambda i: (0, i))
    return pl.pallas_call(
        attend_back_kernel,
        grid=(rows // BLOCK,),
        in_specs=[
            whole,
            part,
            part,
            pl.BlockSpec((width // HEAD, BLOCK), lambda i: (0, i)),
            pl.BlockSpec((rows, BLOCK), lambda i: (0, 0)),
            row,
            row,
            part,
            part,
        ],
        out_specs=[whole, pl.BlockSpec((1, cols), lambda i: (0, 0))],
        out_shape=[
            jax.ShapeDtypeStruct((rows, cols), jnp.bfloat16),
            jax.ShapeDtypeStruct((1, cols), jnp.float32),
        ],
        scratch_shapes=[pltpu.VMEM((rows, cols), jnp.float32)],
        name="attend_back",
    )(qkv, att, grads, lse, key_idx, row_idx, row_first, cos_wide, sin_wide)


def heads_kernel(at_ref, proj_ref, bias_ref, cos_ref, sin_ref, out_ref):
    part = pl.program_id(0)
    val = proj_ref[...] + bias_ref[...]

    @pl.when(part < 2)
    def _():
        out_ref[...] = turn(val, cos_ref, sin_ref, 1.0).astype(jnp.bfloat16)

    @pl.when(part == 2)
    def _():
        out_ref[...] = val.astype(jnp.bfloat16)


def heads_of(proj, bias, cos_wide, sin_wide, at, groups):
    rows = proj.shape[0]
    width = cos_wide.shape[1]
    tab = pl.BlockSpec((rows, width), lambda p, at_ref: (0, 0))
    return pl.pallas_call(
        heads_kernel,
        grid_spec=pltpu.PrefetchScalarGridSpec(
            num_scalar_prefetch=1,
            grid=(3,),
            in_specs=[
                pl.BlockSpec((rows, width), lambda p, at_ref: (0, p * groups + at_ref[0])),
                pl.BlockSpec((1, width), lambda p, at_ref: (0, p * groups + at_ref[0])),
                tab,
                tab,
            ],
            out_specs=pl.BlockSpec((rows, width), lambda p, at_ref: (0, p)),
        ),
        out_shape=jax.ShapeDtypeStruct((rows, 3 * width), jnp.bfloat16),
        name="heads_of",
    )(at[None], proj, bias, cos_wide, sin_wide)


def weight_kernel(at_ref, qkv_ref, fc1_ref, out_ref):
    cols = qkv_ref.shape[3]
    for part in range(3):
        out_ref[:, part * cols : (part + 1) * cols] = qkv_ref[0, :, part, :]
    out_ref[:, 3 * cols :] = fc1_ref[0]


def weight_half(qkv_weight, fc1_weight, layer, half):
    rows = qkv_weight.shape[1]
    qkv_cols = qkv_weight.shape[3] // 2
    fc_cols = fc1_weight.shape[2] // 2
    step = rows // 2
    return pl.pallas_call(
        weight_kernel,
        grid_spec=pltpu.PrefetchScalarGridSpec(
            num_scalar_prefetch=1,
            grid=(2,),
            in_specs=[
                pl.BlockSpec((1, step, 3, qkv_cols), lambda i, at_ref: (layer, i, 0, at_ref[0])),
                pl.BlockSpec((1, step, fc_cols), lambda i, at_ref: (layer, i, at_ref[0])),
            ],
            out_specs=pl.BlockSpec((step, 3 * qkv_cols + fc_cols), lambda i, at_ref: (i, 0)),
        ),
        out_shape=jax.ShapeDtypeStruct((rows, 3 * qkv_cols + fc_cols), jnp.bfloat16),
        name="weight_half",
    )(half[None], qkv_weight, fc1_weight)


def tie(vals):
    return lax.optimization_barrier(vals)


def pick(index, parts):
    on = index == 1
    return (jnp.where(on, parts[1], parts[0]), jnp.where(on, parts[0], parts[1]))


def order_two(index, own, other, axis):
    on = index == 1
    first = jnp.where(on, other, own)
    second = jnp.where(on, own, other)
    return jnp.concatenate([first, second], axis=axis)


def gather_first(piece, place):
    along_x = [place.to_hi(piece, dx) for dx in range(1, place.X)]
    along_f = [place.to_f(piece, df) for df in range(1, place.F)]
    return [piece] + along_x, along_f


def gather_second(along_x, along_f, place, axis):
    split = split_rows if axis == 0 else split_cols
    out = list(along_x)
    for df in range(1, place.F):
        out.append(along_f[df - 1])
        for dx in range(1, place.X):
            out.append(place.to_f(split(along_x[dx], 2)[0], df))
            out.append(place.to_hi(split(along_f[df - 1], 2)[1], dx))
    return out


def scatter_first(chunk, place, x_first):
    low = jnp.bfloat16
    if x_first:
        return [
            [place.to_hi(chunk(df, dx).astype(low), dx) for dx in range(1, place.X)]
            for df in range(place.F)
        ]
    return [
        [place.to_f(chunk(df, dx).astype(low), df) for df in range(1, place.F)]
        for dx in range(place.X)
    ]


def scatter_second(chunk, got, place, x_first):
    low = jnp.bfloat16
    sums = []
    for i, parts in enumerate(got):
        total = chunk(i, 0) if x_first else chunk(0, i)
        for part in parts:
            total = total + part.astype(jnp.float32)
        sums.append(total)
    send = place.to_f if x_first else place.to_hi
    return sums[0], [send(sums[d].astype(low), d) for d in range(1, len(sums))]


def scatter_last(own, got):
    for part in got:
        own = own + part.astype(jnp.float32)
    return own


def sum_all(val, place, axes):
    for axis in axes:
        size = lax.axis_size(axis)
        dist = 1
        while dist < size:
            val = val + lax.ppermute(val, axis, [(i, i ^ dist) for i in range(size)])
            dist *= 2
    return val


def gather_tensor(piece, place):
    return jnp.concatenate(
        [piece] + [place.to_t(piece, d) for d in range(1, place.T)], axis=0
    )


def pair_rows(partial, place):
    own, other = split_rows(partial, 2)
    return own + place.to_lo(other)


def reduce_tensor(pair_sum, place, wire):
    chunks = split_rows(pair_sum, place.T)
    total = chunks[0]
    for d in range(1, place.T):
        total = total + place.to_t(chunks[d].astype(wire), d).astype(jnp.float32)
    return total


def with_partner(rows, place):
    return jnp.concatenate([rows, place.to_lo(rows)], axis=0)


def swap_heads(val, place, parts):
    groups = split_cols(val, parts)
    picked = [xor_order(split_cols(g, place.X), place.hi) for g in groups]
    out = []
    for dx in range(place.X):
        piece = jnp.concatenate([p[dx] for p in picked], axis=1)
        out.append(piece if dx == 0 else place.to_hi(piece, dx))
    return jnp.concatenate(out, axis=0)


def unswap_heads(val, place, parts):
    rows = split_rows(val, place.X)
    got = [rows[0]] + [place.to_hi(rows[dx], dx) for dx in range(1, place.X)]
    split = [split_cols(piece, parts) for piece in got]
    out = []
    for part in range(parts):
        out += xor_order([split[dx][part] for dx in range(place.X)], place.hi)
    return jnp.concatenate(out, axis=1)


def norm_rows(hidden):
    row_mean = jnp.mean(hidden, axis=1, keepdims=True)
    centred = hidden - row_mean
    inv_std = lax.rsqrt(jnp.mean(centred * centred, axis=1, keepdims=True) + LN_EPS)
    return (centred * inv_std, inv_std)


def shards(
    layer_input,
    doc_lengths,
    ln_gain,
    ln_shift,
    qkv_weight,
    qkv_bias,
    out_weight,
    out_bias,
    fc1_weight,
    fc1_bias,
    fc2_weight,
    fc2_bias,
    cotangent,
):
    place = Place()
    F, X, T = place.F, place.X, place.T
    low = jnp.bfloat16
    layers = ln_gain.shape[0]
    tok_rows = layer_input.shape[0]
    pack_rows = tok_rows * place.C
    own_rows = tok_rows // T
    qkv_cols = qkv_weight.shape[3] // 2
    fc_cols = fc1_weight.shape[2] // 2
    head_cols = qkv_cols // X
    qkv_all = 3 * qkv_cols

    tok_idx = token_index(place, tok_rows)
    doc_end = jnp.cumsum(doc_lengths[0])
    passed = (tok_idx[:, None] >= doc_end[None, :]).astype(jnp.int32)
    tok_first = jnp.sum(passed * doc_lengths[0][None, :], axis=1)
    tok_pos = tok_idx - tok_first
    key_idx = jnp.broadcast_to(tok_idx[:, None], (pack_rows, BLOCK))
    row_idx, row_first = tok_idx[None, :], tok_first[None, :]
    cos_pack, sin_pack = rope_wide(tok_pos, head_cols // HEAD)
    cos_own, sin_own = cos_pack[: 2 * tok_rows], sin_pack[: 2 * tok_rows]

    gain_rel = rel_cols(ln_gain, place)
    shift_rel = rel_cols(ln_shift, place)
    bias_rel = rel_cols(out_bias + fc2_bias, place)

    def a_piece_of(n, qkv_w, fc1_w):
        own = weight_half(qkv_w, fc1_w, n, place.lo)
        other = weight_half(qkv_w, fc1_w, n, 1 - place.lo)
        return order_two(place.lo, own, place.to_lo(other), 0)

    def b_piece_of(out_w, fc2_w):
        out_own, out_other = pick(place.lo, split_rows(out_w, 2))
        fc2_own, fc2_other = pick(place.lo, split_rows(fc2_w, 2))
        own = jnp.concatenate([out_own, fc2_own], axis=0)
        other = jnp.concatenate([out_other, fc2_other], axis=0)
        return order_two(place.lo, own, place.to_lo(other), 1)

    def own_part(val):
        return lax.dynamic_slice_in_dim(val, place.t * own_rows, own_rows, 0)

    pieces = []
    a_first, b_first, a_all, b_all = [], [], [], []
    source = (qkv_weight, fc1_weight, out_weight, fc2_weight)
    hold = None
    for n in range(layers):
        qkv_w, fc1_w, out_w, fc2_w = source
        a_piece = a_piece_of(n, qkv_w, fc1_w)
        if n > 0:
            a_piece, hold = tie((a_piece, hold))
        a_got = gather_first(a_piece, place)
        if n == 0:
            a_got, source = tie((a_got, source))
            qkv_w, fc1_w, out_w, fc2_w = source
        a_chunks = gather_second(a_got[0], a_got[1], place, 0)
        b_piece = b_piece_of(out_w[n], fc2_w[n])
        if n == 0:
            b_piece, a_chunks = tie((b_piece, a_chunks))
        else:
            b_piece, a_got = tie((b_piece, a_got))
        b_got = gather_first(b_piece, place)
        b_got, hold = tie((b_got, b_piece))
        b_chunks = gather_second(b_got[0], b_got[1], place, 1)
        a_first.append(a_got)
        b_first.append(b_got)
        a_all.append(a_chunks)
        b_all.append(b_chunks)

    def mix_cols(cols, chunks, combine, axis):
        at, out = 0, None
        for chunk in chunks:
            size = chunk.shape[axis]
            step = combine(cols[:, at : at + size], chunk)
            out = step if out is None else out + step
            at += size
        return out

    hidden = rel_cols(own_part(layer_input), place)
    full = rel_cols(rel_rows(layer_input, place), place)
    stored = []
    summed_last = None
    for n in range(layers):
        a_chunks = a_all[n]
        normed, inv_std = norm_rows(hidden)
        if n == 0:
            full_norm, full_inv = norm_rows(full)
            normal_tok = (full_norm * gain_rel[n] + shift_rel[n]).astype(low)
        else:
            normal_tok = gather_tensor((normed * gain_rel[n] + shift_rel[n]).astype(low), place)
        normal_in = with_partner(normal_tok, place)
        own_bias, other_bias = pick(place.lo, split_cols(qkv_bias[n], 2))
        own_b1, other_b1 = pick(place.lo, split_cols(fc1_bias[n], 2))
        proj = mix_cols(normal_in, a_chunks, lambda u, w: matmul(u, w[:, :qkv_all]), 0)
        bias_row = own_bias.reshape(1, qkv_all)
        got_heads = [
            heads_of(proj, bias_row, cos_own, sin_own, place.hi ^ dx, X) for dx in range(X)
        ]
        for dx in range(1, X):
            got_heads[dx] = place.to_hi(got_heads[dx], dx)
        preact = mix_cols(normal_in, a_chunks, lambda u, w: matmul(u, w[:, qkv_all:]), 0) + own_b1
        gelu_out = gelu_value(preact).astype(low)
        grouped = jnp.concatenate(got_heads, axis=0)
        att_heads, lse = attend(grouped, key_idx, row_idx, row_first)
        att_tok = unswap_heads(att_heads, place, 1)
        mixed = jnp.concatenate([att_tok, gelu_out], axis=1)
        stored.append((normed, inv_std, normal_in, grouped, att_heads, lse, preact, mixed))
        partial = jnp.concatenate([matmul(mixed, chunk) for chunk in b_all[n]], axis=1)
        pair_sum = pair_rows(partial, place)
        if n < layers - 1:
            summed = reduce_tensor(pair_sum, place, jnp.float32)
            hidden = hidden + summed + bias_rel[n]
            hidden, a_first[n + 1] = tie((hidden, a_first[n + 1]))

    upstream = rel_cols(own_part(cotangent), place)
    up_tok = rel_cols(rel_rows(cotangent, place), place).astype(low)
    small = [[None] * layers for column in range(5)]
    big = [[None] * layers for column in range(4)]
    pending = None
    for n in reversed(range(layers)):
        a_chunks, b_chunks = a_all[n], b_all[n]
        normed, inv_std, normal_in, grouped, att_heads, lse, preact, mixed = stored[n]
        if n != layers - 1:
            up_tok = gather_tensor(upstream.astype(low), place)
            pair_sum, up_tok = tie((pair_sum, up_tok))
        up_low = with_partner(up_tok, place)
        if pending is not None:
            up_low, pending = tie((up_low, pending))
        if n == 0 or layers == 1:
            summed = reduce_tensor(pair_sum, place, low)
            final = hidden + summed + bias_rel[layers - 1]
            layer_output = rel_cols(rel_rows(gather_tensor(final, place), place), place)
        normal_cols = split_cols(normal_in, F * X)
        up_cols = split_cols(up_low, F * X)
        grad_obias = jnp.sum(upstream, axis=0)

        grad_mixed = mix_cols(up_low, b_chunks, contract_cols, 1)
        grad_att = grad_mixed[:, :qkv_cols].astype(low)
        grad_heads = swap_heads(grad_att, place, 1)
        grad_pre = grad_mixed[:, qkv_cols:] * gelu_slope(preact)
        grad_b1 = jnp.sum(grad_pre, axis=0)
        grad_pre_low = grad_pre.astype(low)

        def b_chunk(df, dx):
            return contract_rows(mixed, up_cols[df * X + dx])

        def fc1_chunk(df, dx):
            return contract_rows(normal_cols[df * X + dx], grad_pre_low)

        b_got = scatter_first(b_chunk, place, True)
        fc1_got = scatter_first(fc1_chunk, place, False)

        grad_proj, qbias_own = attend_back(
            grouped, att_heads, grad_heads, lse, key_idx, row_idx, row_first, cos_pack, sin_pack
        )
        grad_proj_tok = unswap_heads(grad_proj, place, 3)
        grad_proj_tok, b_got = tie((grad_proj_tok, b_got))
        b_own, b_sent = scatter_second(b_chunk, b_got, place, True)

        def qkv_chunk(df, dx):
            return contract_rows(normal_cols[df * X + dx], grad_proj_tok)

        grad_in = jnp.concatenate(
            [
                contract_cols(grad_proj_tok, chunk[:, :qkv_all])
                + contract_cols(grad_pre_low, chunk[:, qkv_all:])
                for chunk in a_chunks
            ],
            axis=1,
        )
        pair_grad = pair_rows(grad_in, place)
        qkv_got = scatter_first(qkv_chunk, place, True)
        pair_grad, fc1_got = tie((pair_grad, fc1_got))
        fc1_own, fc1_sent = scatter_second(fc1_chunk, fc1_got, place, False)
        grad_norm_out = reduce_tensor(pair_grad, place, low)
        grad_norm_out, b_sent, qkv_got = tie((grad_norm_out, b_sent, qkv_got))
        qkv_own, qkv_sent = scatter_second(qkv_chunk, qkv_got, place, True)
        pending = (fc1_sent, qkv_sent)

        grad_gain = jnp.sum(grad_norm_out * normed, axis=0)
        grad_shift = jnp.sum(grad_norm_out, axis=0)
        grad_normed = grad_norm_out * gain_rel[n]
        upstream = upstream + inv_std * (
            grad_normed
            - jnp.mean(grad_normed, axis=1, keepdims=True)
            - normed * jnp.mean(grad_normed * normed, axis=1, keepdims=True)
        )

        b_grad = scatter_last(b_own, b_sent)
        fc1_grad = scatter_last(fc1_own, fc1_sent)
        qkv_grad = scatter_last(qkv_own, qkv_sent)
        in_rows = qkv_weight.shape[1]
        own, other = pick(place.lo, split_rows(qkv_grad, 2))
        got = place.to_lo(other)
        big[0][n] = order_two(
            place.lo, own.reshape(in_rows, 3, qkv_cols), got.reshape(in_rows, 3, qkv_cols), 2
        )
        own, other = pick(place.lo, split_rows(fc1_grad, 2))
        big[2][n] = order_two(place.lo, own, place.to_lo(other), 1)
        own, other = pick(place.lo, split_cols(b_grad, 2))
        got = place.to_lo(other)
        big[1][n] = order_two(place.lo, own[:qkv_cols], got[:qkv_cols], 0)
        big[3][n] = order_two(place.lo, own[qkv_cols:], got[qkv_cols:], 0)
        grad_qbias = lax.dynamic_update_slice(
            jnp.zeros(qkv_bias.shape[1:], jnp.float32),
            qbias_own.reshape(3, head_cols),
            (jnp.zeros((), jnp.int32), place.lo * qkv_cols + place.hi * head_cols),
        )
        grad_b1_full = lax.dynamic_update_slice(
            jnp.zeros(fc1_bias.shape[1:], jnp.float32), grad_b1, (place.lo * fc_cols,)
        )
        found = (grad_gain, grad_shift, grad_obias, grad_qbias, grad_b1_full)
        for column in range(5):
            small[column][n] = found[column]

    input_grad = rel_cols(
        rel_rows(gather_tensor(upstream.astype(low), place), place).astype(jnp.float32), place
    )
    wide = jnp.concatenate([rel_cols(jnp.stack(small[i]), place) for i in range(3)], axis=0)
    wide = sum_all(wide, place, ("context", "fsdp", "tensor"))
    gain_total, shift_total, obias_total = [
        wide[i * layers : (i + 1) * layers] for i in range(3)
    ]
    narrow = jnp.concatenate(
        [jnp.stack(small[3]).reshape(layers, 6 * qkv_cols), jnp.stack(small[4])], axis=1
    )
    narrow = sum_all(narrow, place, ("context", "fsdp"))
    qbias_total = narrow[:, : 6 * qkv_cols].reshape(qkv_bias.shape)
    fbias_total = narrow[:, 6 * qkv_cols :]
    return (
        layer_output,
        input_grad,
        gain_total,
        shift_total,
        jnp.stack(big[0]),
        qbias_total,
        jnp.stack(big[1]),
        obias_total,
        jnp.stack(big[2]),
        fbias_total,
        jnp.stack(big[3]),
        obias_total,
    )


def solution(mesh):
    return jax.shard_map(
        shards,
        mesh=mesh,
        in_specs=(
            P(("fsdp", "context"), None),
            P("fsdp", None),
            P(),
            P(),
            P(None, ("fsdp", "context"), None, "tensor"),
            P(None, None, "tensor"),
            P(None, "tensor", ("fsdp", "context")),
            P(),
            P(None, ("fsdp", "context"), "tensor"),
            P(None, "tensor"),
            P(None, "tensor", ("fsdp", "context")),
            P(),
            P(("fsdp", "context"), None),
        ),
        out_specs=(
            P(("fsdp", "context"), None),
            P(("fsdp", "context"), None),
            P(),
            P(),
            P(None, ("fsdp", "context"), None, "tensor"),
            P(None, None, "tensor"),
            P(None, "tensor", ("fsdp", "context")),
            P(),
            P(None, ("fsdp", "context"), "tensor"),
            P(None, "tensor"),
            P(None, "tensor", ("fsdp", "context")),
            P(),
        ),
        check_vma=False,
    )
```
